1024 devices in a mesh: dp: 16 (over z, core), ctx: 64 (over y, x).
Axes of the slice: x: 8, y: 8, z: 8, core: 2. Of those that a mesh axis runs over, the one named last changes fastest.
Arguments:
- query_rows: bfloat16 [16, 8192, 2048], P('dp', 'ctx'), may hold values from -72 to 72
- key_rows: bfloat16 [16, 8192, 512], P('dp', 'ctx'), may hold values from -4 to 4
- value_rows: bfloat16 [16, 8192, 512], P('dp', 'ctx'), may hold values from -6 to 6
- grad_rows: bfloat16 [16, 8192, 2048], P('dp', 'ctx'), may hold values from -6 to 6
- bucket_rank: int32 [16, 8192], P('dp', 'ctx'), may hold values from 0 to 255, as said below
- sample_rows: int32 [16, 64], P('dp', 'ctx'), may hold values from 0 to 127, as said below
- sample_count: int32 [16, 64], P('dp', 'ctx'), may hold values from 1 to 3
- sink_logit: float32 [16], replicated, may hold values from 3 to 6
Outputs:
- query_grad: bfloat16 [16, 8192, 2048], P('dp', 'ctx')
- key_grad: bfloat16 [16, 8192, 512], P('dp', 'ctx')
- value_grad: bfloat16 [16, 8192, 512], P('dp', 'ctx')
- sink_grad: float32 [16], replicated
The draws below stay inside these ranges and needn't reach their ends.
Inputs may be any that keep to these rules, and one draw needn't show every extreme that they name: `bucket_rank`: for every sequence and every m, the values over the 256 tokens held by ctx indices 2m and 2m+1 are a permutation of 0 to 255. `sample_rows`: slot c names a row of the 128 tokens held by ctx index c, counted from that block's first token; the slots of one block name distinct rows.
All inputs are finite; a program needn't handle non-finite values.
Results may differ from the reference program's by a relative error of at most 0.0075.
Values may be sent and summed in bfloat16 or wider, within the bound.
A program may use at most 32 MiB of HBM per device.

```python
from functools import partial
import jax
import jax.numpy as jnp
from jax import lax

HEADS = 16
KV_HEADS = 4
HDIM = 128
BUCKET = 128
TOK_DEV = 128
SAMP_DEV = 1
SEQS = 16
TOKENS = 8192
SAMPLES = 64


def query_key_pair(key):
    base = jax.random.fold_in(key, 4242)
    key_stream, query_stream = jax.random.split(base, 2)
    key_values = jax.random.truncated_normal(key_stream, -4.0, 4.0, (SEQS, TOKENS, KV_HEADS * HDIM), jnp.float32)
    query_values = jax.random.truncated_normal(query_stream, -4.0, 4.0, (SEQS, TOKENS, HEADS * HDIM), jnp.float32)
    return (query_values, key_values)


def draw_query_rows(key, part):
    return query_key_pair(key)[0].astype(jnp.bfloat16)


def draw_key_rows(key, part):
    return query_key_pair(key)[1].astype(jnp.bfloat16)


def draw_bucket_rank(key, part):
    pairs = TOKENS // (2 * TOK_DEV)
    streams = jax.random.split(jax.random.fold_in(key, 77), SEQS * pairs)
    orders = jax.vmap(lambda one_key: jax.random.permutation(one_key, 2 * TOK_DEV))(streams)
    return orders.reshape(SEQS, TOKENS).astype(jnp.int32)


def draw_sample_rows(key, part):
    blocks = TOKENS // TOK_DEV
    streams = jax.random.split(jax.random.fold_in(key, 91), SEQS * blocks)
    chosen = jax.vmap(lambda one_key: jax.random.permutation(one_key, TOK_DEV)[:SAMP_DEV])(streams)
    return chosen.reshape(SEQS, SAMPLES).astype(jnp.int32)


def with_ends(result, rng, smallest, top_value):
    spot = [jax.random.randint(jax.random.fold_in(rng, axis), (), 0, length) for axis, length in enumerate(result.shape)]
    widest = result.shape.index(max(result.shape))
    next_to = spot[:widest] + [(spot[widest] + 1) % result.shape[widest]] + spot[widest + 1:]
    return result.at[tuple(spot)].set(smallest).at[tuple(next_to)].set(top_value)


def block_levels(stream_key, shape, shards, least, top_value):
    def one(dim, blocks):
        steps = jax.random.uniform(jax.random.fold_in(jax.random.fold_in(stream_key, 6), dim), (blocks,), jnp.float32, least / len(shards), top_value / len(shards))
        return jnp.repeat(jnp.exp(steps), shape[dim] // blocks).reshape((-1,) + (1,) * (len(shape) - dim - 1))

    factor_of = one(*shards[0])
    for cut in shards[1:]:
        factor_of = factor_of * one(*cut)
    return factor_of


def normal_values(rng, dims, scale, bound, cuts=(), held_as=jnp.bfloat16):
    values = scale * jax.random.normal(rng, dims, jnp.float32)
    if cuts:
        values = values * block_levels(rng, dims, cuts, -0.22, 0.18)
    return jnp.clip(values, -bound, bound).astype(held_as)


def setup_inputs(seed: int = 0) -> dict:
    splits = jax.random.split(jax.random.key(seed), 9)
    return {
        "query_rows": draw_query_rows(jax.random.fold_in(splits[8], 71), 0),
        "key_rows": draw_key_rows(jax.random.fold_in(splits[8], 71), 0),
        "value_rows": normal_values(splits[2], (SEQS, TOKENS, KV_HEADS * HDIM), 1.0, 6.0, ((0, 16), (1, 64))),
        "grad_rows": normal_values(splits[3], (SEQS, TOKENS, HEADS * HDIM), 1.0, 6.0, ((0, 16), (1, 64))),
        "bucket_rank": draw_bucket_rank(jax.random.fold_in(splits[8], 71), 0),
        "sample_rows": draw_sample_rows(jax.random.fold_in(splits[8], 71), 0),
        "sample_count": with_ends(jax.random.randint(splits[6], (SEQS, SAMPLES), 1, 4), jax.random.fold_in(splits[6], 1), 1, 3).astype(jnp.int32),
        "sink_logit": jnp.clip(jax.random.uniform(splits[7], (HEADS,), jnp.float32, 3.0, 6.0), 3.0, 6.0),
    }


def one_sequence(items, sink_logit):
    query_seq, key_seq, value_seq, grad_seq, rank_seq, rows_seq, count_seq = items
    per_group = HEADS // KV_HEADS
    kv_width = KV_HEADS * HDIM
    score_scale = HDIM ** -0.5
    span = 2 * TOK_DEV
    blocks = TOKENS // span
    per_block = span // BUCKET
    token_index = jnp.arange(TOKENS, dtype=jnp.int32)
    position = (token_index // span) * span + rank_seq.astype(jnp.int32)
    ordered = jnp.zeros((TOKENS,), jnp.int32).at[position].set(token_index)
    slot_token = (jnp.arange(SAMPLES, dtype=jnp.int32) // SAMP_DEV) * TOK_DEV + rows_seq.astype(jnp.int32)
    slot_bucket = position[slot_token] // BUCKET
    log_weight = jnp.log(count_seq.astype(jnp.float32))
    sample_keys = key_seq[slot_token].astype(jnp.float32).reshape(SAMPLES, KV_HEADS, HDIM)
    sample_values = value_seq[slot_token].astype(jnp.float32).reshape(SAMPLES, KV_HEADS, HDIM)
    sink_row = sink_logit.reshape(KV_HEADS, per_group)
    sorted_query = query_seq[ordered].reshape(blocks, span, KV_HEADS, per_group, HDIM)
    sorted_keys = key_seq[ordered].reshape(blocks, span, KV_HEADS, HDIM)
    sorted_values = value_seq[ordered].reshape(blocks, span, KV_HEADS, HDIM)
    sorted_grads = grad_seq[ordered].reshape(blocks, span, KV_HEADS, per_group, HDIM)
    firsts = jnp.arange(blocks, dtype=jnp.int32) * span

    def block_pass(block_items):
        block_query, block_keys, block_values, block_grads, first_row = block_items
        query_flat = block_query.astype(jnp.float32)
        grad_flat = block_grads.astype(jnp.float32)
        query_bucket = (first_row + jnp.arange(span, dtype=jnp.int32)) // BUCKET
        query_split = query_flat.reshape(per_block, BUCKET, KV_HEADS, per_group, HDIM)
        grad_split = grad_flat.reshape(per_block, BUCKET, KV_HEADS, per_group, HDIM)
        key_split = block_keys.astype(jnp.float32).reshape(per_block, BUCKET, KV_HEADS, HDIM)
        value_split = block_values.astype(jnp.float32).reshape(per_block, BUCKET, KV_HEADS, HDIM)
        bucket_score = jnp.einsum("nikgd,njkd->nikgj", query_split, key_split) * score_scale
        bucket_score = bucket_score.reshape(span, KV_HEADS, per_group, BUCKET)
        sample_score = jnp.einsum("tkgd,ckd->tkgc", query_flat, sample_keys) * score_scale + log_weight
        excluded = query_bucket[:, None] == slot_bucket[None, :]
        sample_score = jnp.where(excluded[:, None, None, :], -jnp.inf, sample_score)
        row_max = jnp.maximum(jnp.maximum(jnp.max(bucket_score, -1), jnp.max(sample_score, -1)), sink_row)
        denominator = (jnp.exp(sink_row - row_max)
                       + jnp.sum(jnp.exp(bucket_score - row_max[..., None]), -1)
                       + jnp.sum(jnp.exp(sample_score - row_max[..., None]), -1))
        log_total = row_max + jnp.log(denominator)
        bucket_prob = jnp.exp(bucket_score - log_total[..., None])
        sample_prob = jnp.exp(sample_score - log_total[..., None])
        sink_prob = jnp.exp(sink_row - log_total)
        bucket_half = bucket_prob.astype(jnp.bfloat16).astype(jnp.float32)
        sample_half = sample_prob.astype(jnp.bfloat16).astype(jnp.float32)
        bucket_half_split = bucket_half.reshape(per_block, BUCKET, KV_HEADS, per_group, BUCKET)
        out_bucket = jnp.einsum("nikgj,njkd->nikgd", bucket_half_split, value_split).reshape(span, KV_HEADS, per_group, HDIM)
        out_sample = jnp.einsum("tkgc,ckd->tkgd", sample_half, sample_values)
        attended = (out_bucket + out_sample).astype(jnp.bfloat16).astype(jnp.float32)
        delta = jnp.sum(grad_flat * attended, -1)
        bucket_up = jnp.einsum("nikgd,njkd->nikgj", grad_split, value_split).reshape(span, KV_HEADS, per_group, BUCKET)
        sample_up = jnp.einsum("tkgd,ckd->tkgc", grad_flat, sample_values)
        bucket_ds = (bucket_prob * (bucket_up - delta[..., None])).astype(jnp.bfloat16).astype(jnp.float32)
        sample_ds = (sample_prob * (sample_up - delta[..., None])).astype(jnp.bfloat16).astype(jnp.float32)
        bucket_ds_split = bucket_ds.reshape(per_block, BUCKET, KV_HEADS, per_group, BUCKET)
        query_part = score_scale * (jnp.einsum("nikgj,njkd->nikgd", bucket_ds_split, key_split).reshape(span, KV_HEADS, per_group, HDIM)
                                    + jnp.einsum("tkgc,ckd->tkgd", sample_ds, sample_keys))
        key_part = score_scale * jnp.einsum("nikgj,nikgd->njkd", bucket_ds_split, query_split).reshape(span, KV_HEADS, HDIM)
        value_part = jnp.einsum("nikgj,nikgd->njkd", bucket_half_split, grad_split).reshape(span, KV_HEADS, HDIM)
        key_slot = score_scale * jnp.einsum("tkgc,tkgd->ckd", sample_ds, query_flat)
        value_slot = jnp.einsum("tkgc,tkgd->ckd", sample_half, grad_flat)
        sink_part = -jnp.sum(sink_prob * delta, 0)
        return query_part, key_part, value_part, key_slot, value_slot, sink_part

    query_part, key_part, value_part, key_slot, value_slot, sink_part = lax.map(
        block_pass, (sorted_query, sorted_keys, sorted_values, sorted_grads, firsts))
    query_grad = query_part.reshape(TOKENS, HEADS * HDIM)[position].astype(jnp.bfloat16)
    key_slot_sum = jnp.sum(key_slot, 0).reshape(SAMPLES, kv_width)
    value_slot_sum = jnp.sum(value_slot, 0).reshape(SAMPLES, kv_width)
    key_grad = (key_part.reshape(TOKENS, kv_width)[position]
                + jnp.zeros((TOKENS, kv_width), jnp.float32).at[slot_token].add(key_slot_sum)).astype(jnp.bfloat16)
    value_grad = (value_part.reshape(TOKENS, kv_width)[position]
                  + jnp.zeros((TOKENS, kv_width), jnp.float32).at[slot_token].add(value_slot_sum)).astype(jnp.bfloat16)
    return query_grad, key_grad, value_grad, jnp.sum(sink_part, 0).reshape(HEADS)


def reference(query_rows, key_rows, value_rows, grad_rows, bucket_rank, sample_rows, sample_count, sink_logit):
    results = lax.map(partial(one_sequence, sink_logit=sink_logit),
                      (query_rows, key_rows, value_rows, grad_rows, bucket_rank, sample_rows, sample_count))
    return results[0], results[1], results[2], jnp.sum(results[3], 0)
```

```python
import functools

import jax
import jax.numpy as jnp
from jax import lax
from jax.experimental import pallas as pl
from jax.experimental.pallas import tpu as pltpu
from jax.sharding import PartitionSpec as P

HEADS = 16
KV_HEADS = 4
HDIM = 128
BUCKET = 128
GROUP = HEADS // KV_HEADS
WIDTH = KV_HEADS * HDIM
ROW = 2 * WIDTH + 128
NEG = -1e30
MESH = pl.DeviceIdType.MESH


def whole_kernel(
    ny, nx, ndp,
    q_ref, k_ref, v_ref, g_ref, rank_ref, rows_ref, count_ref, sink_ref,
    dq_ref, dk_ref, dv_ref, ds_ref,
    row_buf, rows1, blk_buf, samples, far_k, far_v, far_rank,
    prob, dscore, own_k, own_v, back_buf, back, terms, terms_in, lines, lines_in,
    sink_buf, sink_dp, sink_part, sink_y,
    x_send, x_recv, y_send, y_recv, pair_send, pair_recv,
    back_send, back_recv, t_send, t_recv, l_send, l_recv,
    sd_send, sd_recv, sy_send, sy_recv,
):
    f32, bf16 = jnp.float32, jnp.bfloat16
    length = k_ref.shape[0]
    slots = ny * nx
    keys = 2 * length + slots
    scale = HDIM ** (-0.5)
    ctx, dp = lax.axis_index("ctx"), lax.axis_index("dp")
    y, x = ctx // nx, ctx % nx

    def x_peer(d):
        return {"ctx": y * nx + (x + d) % nx}

    def y_peer(d):
        return {"ctx": ((y + d) % ny) * nx + x}

    def dp_peer(d):
        return {"dp": (dp + d) % ndp}

    partner = {"ctx": y * nx + x + 1 - 2 * (x % 2)}
    started = []

    def send(src, dst, ssem, rsem, device):
        copy = pltpu.make_async_remote_copy(
            src_ref=src, dst_ref=dst, send_sem=ssem, recv_sem=rsem,
            device_id=device, device_id_type=MESH,
        )
        copy.start()
        started.append(copy)
        return copy

    barrier = pltpu.get_barrier_semaphore()
    peers = (
        [x_peer(d) for d in range(1, nx)]
        + [y_peer(d) for d in range(1, ny)]
        + [dp_peer(d) for d in range(1, ndp)]
    )
    for peer in peers:
        pl.semaphore_signal(barrier, inc=1, device_id=peer, device_id_type=MESH)

    lane = lax.broadcasted_iota(jnp.int32, (8, length), 1)
    picked = rows_ref[...]
    hit = lane == picked
    one_hot = jnp.where(hit, 1.0, 0.0).astype(bf16)
    own_row = rank_ref[...]
    own_bucket = jnp.where(own_row >= BUCKET, 1.0, 0.0)
    mark = jnp.sum(jnp.where(hit, own_bucket, 0.0), axis=1, keepdims=True)
    row_buf[:, :WIDTH] = jnp.dot(one_hot, k_ref[...], preferred_element_type=f32)
    row_buf[:, WIDTH : 2 * WIDTH] = jnp.dot(one_hot, v_ref[...], preferred_element_type=f32)
    tail = lax.broadcasted_iota(jnp.int32, (8, 128), 1)
    row_buf[:, 2 * WIDTH :] = jnp.where(
        tail == 0, count_ref[...].astype(f32), jnp.where(tail == 1, mark, 0.0)
    )
    rows1[pl.ds(x, 1), :] = row_buf[0:1, :]
    pl.semaphore_wait(barrier, len(peers))

    x_copies = [
        send(row_buf.at[pl.ds(0, 1)], rows1.at[pl.ds(x, 1)],
             x_send.at[d - 1], x_recv.at[d - 1], x_peer(d))
        for d in range(1, nx)
    ]
    pair_copies = [
        send(rank_ref, far_rank, pair_send.at[0], pair_recv.at[0], partner),
        send(k_ref, far_k, pair_send.at[1], pair_recv.at[1], partner),
        send(v_ref, far_v, pair_send.at[2], pair_recv.at[2], partner),
    ]
    for copy in x_copies:
        copy.wait_recv()
    blk_buf[...] = rows1[...].astype(bf16)
    samples[y] = rows1[...].astype(bf16)
    y_copies = [
        send(blk_buf, samples.at[y], y_send.at[d - 1], y_recv.at[d - 1], y_peer(d))
        for d in range(1, ny)
    ]
    for copy in pair_copies:
        copy.wait_recv()
    for copy in y_copies:
        copy.wait_recv()

    panel = jnp.concatenate([samples[i].astype(f32) for i in range(ny)], 0)
    panel_kv = panel[:, : 2 * WIDTH].astype(bf16)
    counts = panel[:, 2 * WIDTH : 2 * WIDTH + 1]
    marks = panel[:, 2 * WIDTH + 1 : 2 * WIDTH + 2]
    up = lax.broadcasted_iota(jnp.int32, (length, length), 0)
    across = lax.broadcasted_iota(jnp.int32, (length, length), 1)
    far_bucket = jnp.where(far_rank[...] >= BUCKET, 1.0, 0.0)

    def upright(line):
        return jnp.sum(jnp.where(up == across, line, 0.0), axis=1, keepdims=True)

    key_bucket = jnp.concatenate([upright(own_bucket), upright(far_bucket)], 0)
    slot = lax.broadcasted_iota(jnp.int32, (slots, 1), 0)
    near = jnp.where(slot // 2 == ctx // 2, marks, 2.0)
    bias = jnp.concatenate(
        [
            jnp.where(key_bucket == own_bucket, 0.0, NEG),
            jnp.where(near == own_bucket, NEG, jnp.log(counts)),
        ],
        0,
    )
    bias = jnp.concatenate([bias] * GROUP, 1)

    def heads_of(ref, j):
        first = j * GROUP * HDIM
        return jnp.concatenate(
            [ref[:, first + h * HDIM : first + (h + 1) * HDIM] for h in range(GROUP)], 0
        )

    def keys_of(own, far, offset, j):
        cut = slice(j * HDIM, (j + 1) * HDIM)
        return jnp.concatenate(
            [own[:, cut], far[:, cut], panel_kv[:, offset + j * HDIM : offset + (j + 1) * HDIM]], 0
        )

    transposed = (((1,), (1,)), ((), ()))
    sink_lane = lax.broadcasted_iota(jnp.int32, (1, 128), 1)
    sink_line = jnp.zeros((1, 128), f32)
    for j in range(KV_HEADS):
        score = lax.dot_general(
            keys_of(k_ref, far_k, 0, j), heads_of(q_ref, j), transposed,
            preferred_element_type=f32,
        ) * scale + bias
        sink_row = jnp.concatenate(
            [jnp.full((1, length), sink_ref[j * GROUP + h], f32) for h in range(GROUP)], 1
        )
        top = jnp.maximum(jnp.max(score, axis=0, keepdims=True), sink_row)
        weight = jnp.exp(score - top)
        sink_weight = jnp.exp(sink_row - top)
        inverse = 1.0 / (jnp.sum(weight, axis=0, keepdims=True) + sink_weight)
        chance = weight * inverse
        lift = lax.dot_general(
            keys_of(v_ref, far_v, WIDTH, j), heads_of(g_ref, j), transposed,
            preferred_element_type=f32,
        )
        delta = jnp.sum(chance * lift, axis=0, keepdims=True)
        prob[j] = chance.astype(bf16)
        dscore[j] = (chance * (lift - delta)).astype(bf16)
        sink_term = sink_weight * inverse * delta
        for h in range(GROUP):
            part = jnp.sum(sink_term[:, h * length : (h + 1) * length], axis=1, keepdims=True)
            sink_line = jnp.where(sink_lane == j * GROUP + h, part, sink_line)
    sink_buf[...] = sink_line
    sink_dp[pl.ds(dp, 1), :] = sink_line
    dp_copies = [
        send(sink_buf, sink_dp.at[pl.ds(dp, 1)], sd_send.at[d - 1], sd_recv.at[d - 1], dp_peer(d))
        for d in range(1, ndp)
    ]

    t_copies, back_copies = [], []
    for j in range(KV_HEADS):
        cut = slice(j * HDIM, (j + 1) * HDIM)
        ds_t, p_t = dscore[j], prob[j]
        q_part, g_part = heads_of(q_ref, j), heads_of(g_ref, j)
        key_all = jnp.dot(ds_t, q_part, preferred_element_type=f32) * scale
        value_all = jnp.dot(p_t, g_part, preferred_element_type=f32)
        for i in range(ny):
            low = 2 * length + i * nx
            terms[j, i, :, :HDIM] = key_all[low : low + nx].astype(bf16)
            terms[j, i, :, HDIM:] = value_all[low : low + nx].astype(bf16)
        terms_in[j, y] = terms[j, y]
        for d in range(1, ny):
            t_copies.append(send(
                terms.at[j, (y + d) % ny], terms_in.at[j, y],
                t_send.at[j, d - 1], t_recv.at[j, d - 1], y_peer(d),
            ))
        back_buf[j, :, :HDIM] = key_all[length : 2 * length].astype(bf16)
        back_buf[j, :, HDIM:] = value_all[length : 2 * length].astype(bf16)
        back_copies.append(send(
            back_buf.at[j], back.at[j], back_send.at[j], back_recv.at[j], partner
        ))
        own_k[:, cut] = key_all[:length]
        own_v[:, cut] = value_all[:length]
    for copy in dp_copies:
        copy.wait_recv()
    sink_sum = jnp.sum(sink_dp[...], axis=0, keepdims=True)
    sink_part[...] = sink_sum
    sink_y[pl.ds(y, 1), :] = sink_sum
    sy_copies = [
        send(sink_part, sink_y.at[pl.ds(y, 1)], sy_send.at[d - 1], sy_recv.at[d - 1], y_peer(d))
        for d in range(1, ny)
    ]
    for j in range(KV_HEADS):
        query_part = scale * lax.dot_general(
            dscore[j], keys_of(k_ref, far_k, 0, j), (((0,), (0,)), ((), ())),
            preferred_element_type=f32,
        )
        for h in range(GROUP):
            first = (j * GROUP + h) * HDIM
            dq_ref[:, first : first + HDIM] = query_part[h * length : (h + 1) * length].astype(bf16)
    for copy in t_copies:
        copy.wait_recv()
    for copy in sy_copies:
        copy.wait_recv()
    for j in range(KV_HEADS):
        total = terms_in[j, 0].astype(f32)
        for i in range(1, ny):
            total = total + terms_in[j, i].astype(f32)
        lines[:, j * HDIM : (j + 1) * HDIM] = total[:, :HDIM]
        lines[:, WIDTH + j * HDIM : WIDTH + (j + 1) * HDIM] = total[:, HDIM:]
    lines[:, 2 * WIDTH :] = jnp.broadcast_to(
        jnp.sum(sink_y[...], axis=0, keepdims=True), (nx, 128)
    )
    lines_in[pl.ds(x, 1), :] = lines[pl.ds(x, 1), :]
    l_copies = [
        send(lines.at[pl.ds((x + d) % nx, 1)], lines_in.at[pl.ds(x, 1)],
             l_send.at[d - 1], l_recv.at[d - 1], x_peer(d))
        for d in range(1, nx)
    ]
    for copy in back_copies:
        copy.wait_recv()
    for copy in l_copies:
        copy.wait_recv()
    line = jnp.sum(lines_in[...], axis=0, keepdims=True)
    here = lax.broadcasted_iota(jnp.int32, (length, HDIM), 0) == picked
    for j in range(KV_HEADS):
        cut = slice(j * HDIM, (j + 1) * HDIM)
        dk_ref[:, cut] = (
            own_k[:, cut] + back[j, :, :HDIM].astype(f32) + jnp.where(here, line[:, cut], 0.0)
        ).astype(bf16)
        dv_ref[:, cut] = (
            own_v[:, cut]
            + back[j, :, HDIM:].astype(f32)
            + jnp.where(here, line[:, WIDTH + j * HDIM : WIDTH + (j + 1) * HDIM], 0.0)
        ).astype(bf16)
    ds_ref[...] = -line[:, 2 * WIDTH :]
    for copy in started:
        copy.wait_send()


def on_device(
    ndp, query_rows, key_rows, value_rows, grad_rows, bucket_rank, sample_rows, sample_count, sink_logit
):
    length = query_rows.shape[1]
    slots = lax.axis_size("ctx")
    nx = 8 if slots >= 64 else 2
    ny = slots // nx
    keys = 2 * length + slots
    f32, bf16, i32 = jnp.float32, jnp.bfloat16, jnp.int32
    vmem, dma = pltpu.VMEM, pltpu.SemaphoreType.DMA
    space = pl.BlockSpec(memory_space=pltpu.VMEM)
    dq, dk, dv, ds = pl.pallas_call(
        functools.partial(whole_kernel, ny, nx, ndp),
        out_shape=[
            jax.ShapeDtypeStruct((length, HEADS * HDIM), bf16),
            jax.ShapeDtypeStruct((length, WIDTH), bf16),
            jax.ShapeDtypeStruct((length, WIDTH), bf16),
            jax.ShapeDtypeStruct((1, 128), f32),
        ],
        in_specs=[space] * 7 + [pl.BlockSpec(memory_space=pltpu.SMEM)],
        out_specs=[space] * 4,
        scratch_shapes=[
            vmem((8, ROW), f32),
            vmem((nx, ROW), f32),
            vmem((nx, ROW), bf16),
            vmem((ny, nx, ROW), bf16),
            vmem((length, WIDTH), bf16),
            vmem((length, WIDTH), bf16),
            vmem((1, length), i32),
            vmem((KV_HEADS, keys, GROUP * length), bf16),
            vmem((KV_HEADS, keys, GROUP * length), bf16),
            vmem((length, WIDTH), f32),
            vmem((length, WIDTH), f32),
            vmem((KV_HEADS, length, 2 * HDIM), bf16),
            vmem((KV_HEADS, length, 2 * HDIM), bf16),
            vmem((KV_HEADS, ny, nx, 2 * HDIM), bf16),
            vmem((KV_HEADS, ny, nx, 2 * HDIM), bf16),
            vmem((nx, ROW), f32),
            vmem((nx, ROW), f32),
            vmem((1, 128), f32),
            vmem((ndp, 128), f32),
            vmem((1, 128), f32),
            vmem((ny, 128), f32),
            dma((nx - 1,)), dma((nx - 1,)),
            dma((ny - 1,)), dma((ny - 1,)),
            dma((3,)), dma((3,)),
            dma((KV_HEADS,)), dma((KV_HEADS,)),
            dma((KV_HEADS, ny - 1)), dma((KV_HEADS, ny - 1)),
            dma((nx - 1,)), dma((nx - 1,)),
            dma((ndp - 1,)), dma((ndp - 1,)),
            dma((ny - 1,)), dma((ny - 1,)),
        ],
        compiler_params=pltpu.CompilerParams(
            collective_id=0, has_side_effects=True, vmem_limit_bytes=40 << 20
        ),
    )(
        query_rows[0], key_rows[0], value_rows[0], grad_rows[0],
        bucket_rank, sample_rows, sample_count, sink_logit,
    )
    return dq[None], dk[None], dv[None], ds[0, :HEADS]


def solution(mesh):
    return jax.shard_map(
        functools.partial(on_device, mesh.shape["dp"]),
        mesh=mesh,
        in_specs=(
            P("dp", "ctx", None),
            P("dp", "ctx", None),
            P("dp", "ctx", None),
            P("dp", "ctx", None),
            P("dp", "ctx"),
            P("dp", "ctx"),
            P("dp", "ctx"),
            P(),
        ),
        out_specs=(P("dp", "ctx", None), P("dp", "ctx", None), P("dp", "ctx", None), P()),
        check_vma=False,
    )
```

```python
import functools

import jax
import jax.numpy as jnp
from jax import lax
from jax.experimental import pallas as pl
from jax.experimental.pallas import tpu as pltpu
from jax.sharding import PartitionSpec as P

HEADS = 16
KV_HEADS = 4
HDIM = 128
BUCKET = 128
GROUP = HEADS // KV_HEADS
WIDTH = KV_HEADS * HDIM
ROW = 2 * WIDTH + 128
NEG = -1e30
EARLY = 1
MESH = pl.DeviceIdType.MESH


def whole_kernel(
    ny, nx, ndp,
    q_hbm, k_hbm, v_hbm, g_hbm, rank_hbm, rows_hbm, count_hbm, sink_hbm,
    dq_ref, dk_ref, dv_ref, ds_ref,
    q_ref, k_ref, v_ref, g_ref, rank_ref, rows_ref, count_ref, sink_ref,
    row_buf, rows1, blk_buf, samples, far_k, far_v, far_rank,
    weights, lifts, stats, dscore, own_k, own_v, back_buf, back,
    terms, terms_in, lines, lines_in,
    sink_buf, sink_dp, sink_part, sink_y, sink_last, sink_x,
    in_sem, x_send, x_recv, y_send, y_recv, pair_send, pair_recv,
    back_send, back_recv, t_send, t_recv, l_send, l_recv,
    sd_send, sd_recv, sy_send, sy_recv, sx_send, sx_recv,
):
    f32, bf16 = jnp.float32, jnp.bfloat16
    length = k_ref.shape[0]
    slots = ny * nx
    scale = HDIM ** (-0.5)
    ctx, dp = lax.axis_index("ctx"), lax.axis_index("dp")
    y, x = ctx // nx, ctx % nx

    def x_peer(d):
        return {"ctx": y * nx + (x + d) % nx}

    def y_peer(d):
        return {"ctx": ((y + d) % ny) * nx + x}

    def dp_peer(d):
        return {"dp": (dp + d) % ndp}

    partner = {"ctx": y * nx + x + 1 - 2 * (x % 2)}
    started = []

    def send(src, dst, ssem, rsem, device):
        copy = pltpu.make_async_remote_copy(
            src_ref=src, dst_ref=dst, send_sem=ssem, recv_sem=rsem,
            device_id=device, device_id_type=MESH,
        )
        copy.start()
        started.append(copy)
        return copy

    def arrived(copies):
        for copy in copies:
            copy.wait_recv()

    barrier = pltpu.get_barrier_semaphore()
    peers = (
        [x_peer(d) for d in range(1, nx)]
        + [y_peer(d) for d in range(1, ny)]
        + [dp_peer(d) for d in range(1, ndp)]
    )
    for peer in peers:
        pl.semaphore_signal(barrier, inc=1, device_id=peer, device_id_type=MESH)
    loads = [
        pltpu.make_async_copy(src, dst, in_sem.at[i])
        for i, (src, dst) in enumerate(
            [
                (rank_hbm, rank_ref), (rows_hbm, rows_ref), (count_hbm, count_ref),
                (k_hbm, k_ref), (v_hbm, v_ref), (sink_hbm, sink_ref),
                (q_hbm, q_ref), (g_hbm, g_ref),
            ]
        )
    ]
    for load in loads:
        load.start()
    for load in loads[:5]:
        load.wait()

    picked = rows_ref[0, 0]
    hit = lax.broadcasted_iota(jnp.int32, (8, length), 1) == picked
    one_hot = jnp.where(hit, 1.0, 0.0).astype(bf16)
    own_bucket = jnp.where(rank_ref[...] >= BUCKET, 1.0, 0.0)
    mark = jnp.sum(jnp.where(hit, own_bucket, 0.0), axis=1, keepdims=True)
    row_buf[:, :WIDTH] = jnp.dot(one_hot, k_ref[...], preferred_element_type=f32)
    row_buf[:, WIDTH : 2 * WIDTH] = jnp.dot(one_hot, v_ref[...], preferred_element_type=f32)
    tail = lax.broadcasted_iota(jnp.int32, (8, 128), 1)
    row_buf[:, 2 * WIDTH :] = jnp.where(
        tail == 0, count_ref[0, 0].astype(f32), jnp.where(tail == 1, mark, 0.0)
    )
    rows1[pl.ds(x, 1), :] = row_buf[0:1, :]
    pl.semaphore_wait(barrier, len(peers))

    x_copies = [
        send(row_buf.at[pl.ds(0, 1)], rows1.at[pl.ds(x, 1)],
             x_send.at[d - 1], x_recv.at[d - 1], x_peer(d))
        for d in range(1, nx)
    ]
    pair_copies = [
        send(rank_ref, far_rank, pair_send.at[0], pair_recv.at[0], partner),
        send(k_ref, far_k, pair_send.at[1], pair_recv.at[1], partner),
        send(v_ref, far_v, pair_send.at[2], pair_recv.at[2], partner),
    ]
    for load in loads[5:]:
        load.wait()

    up = lax.broadcasted_iota(jnp.int32, (length, length), 0)
    across = lax.broadcasted_iota(jnp.int32, (length, length), 1)

    def inside(line):
        upright = jnp.sum(jnp.where(up == across, line, 0.0), axis=1, keepdims=True)
        return jnp.concatenate([jnp.where(upright == own_bucket, 0.0, NEG)] * GROUP, 1)

    def heads_of(ref, j):
        first = j * GROUP * HDIM
        return jnp.concatenate(
            [ref[:, first + h * HDIM : first + (h + 1) * HDIM] for h in range(GROUP)], 0
        )

    def across_dot(left, right):
        return lax.dot_general(
            left, right, (((1,), (1,)), ((), ())), preferred_element_type=f32
        )

    def sink_of(j):
        return jnp.concatenate(
            [jnp.full((1, length), sink_ref[j * GROUP + h], f32) for h in range(GROUP)], 1
        )

    def score_block(which, keys, values, bias, j):
        cut = slice(j * HDIM, (j + 1) * HDIM)
        score = across_dot(keys[:, cut], heads_of(q_ref, j)) * scale + bias
        lift = across_dot(values[:, cut], heads_of(g_ref, j))
        top = jnp.max(score, axis=0, keepdims=True)
        weight = jnp.exp(score - top)
        weights[j, which] = weight
        lifts[j, which] = lift
        stats[j, 3 * which : 3 * which + 1] = top
        stats[j, 3 * which + 1 : 3 * which + 2] = jnp.sum(weight, axis=0, keepdims=True)
        stats[j, 3 * which + 2 : 3 * which + 3] = jnp.sum(weight * lift, axis=0, keepdims=True)

    own_bias = inside(own_bucket)
    for j in range(EARLY):
        score_block(0, k_ref, v_ref, own_bias, j)
    arrived(x_copies)
    blk_buf[...] = rows1[...].astype(bf16)
    samples[y] = rows1[...].astype(bf16)
    y_copies = [
        send(blk_buf, samples.at[y], y_send.at[d - 1], y_recv.at[d - 1], y_peer(d))
        for d in range(1, ny)
    ]
    for j in range(EARLY, KV_HEADS):
        score_block(0, k_ref, v_ref, own_bias, j)
    arrived(pair_copies)
    far_bias = inside(jnp.where(far_rank[...] >= BUCKET, 1.0, 0.0))
    for j in range(KV_HEADS):
        score_block(1, far_k, far_v, far_bias, j)
    arrived(y_copies)

    panel = jnp.concatenate([samples[i].astype(f32) for i in range(ny)], 0)
    panel_kv = panel[:, : 2 * WIDTH].astype(bf16)
    counts = panel[:, 2 * WIDTH : 2 * WIDTH + 1]
    marks = panel[:, 2 * WIDTH + 1 : 2 * WIDTH + 2]
    slot = lax.broadcasted_iota(jnp.int32, (slots, 1), 0)
    near = jnp.where(slot // 2 == ctx // 2, marks, 2.0)
    bias = jnp.concatenate([jnp.where(near == own_bucket, NEG, jnp.log(counts))] * GROUP, 1)
    sink_lane = lax.broadcasted_iota(jnp.int32, (1, 128), 1)
    sink_line = jnp.zeros((1, 128), f32)
    t_copies = []
    for j in range(KV_HEADS):
        low = j * HDIM
        q_part, g_part = heads_of(q_ref, j), heads_of(g_ref, j)
        score = across_dot(panel_kv[:, low : low + HDIM], q_part) * scale + bias
        lift = across_dot(panel_kv[:, WIDTH + low : WIDTH + low + HDIM], g_part)
        sink_row = sink_of(j)
        own_top, far_top = stats[j, 0:1], stats[j, 3:4]
        top = jnp.maximum(
            jnp.maximum(own_top, far_top),
            jnp.maximum(jnp.max(score, axis=0, keepdims=True), sink_row),
        )
        weight = jnp.exp(score - top)
        own_part, far_part = jnp.exp(own_top - top), jnp.exp(far_top - top)
        sink_weight = jnp.exp(sink_row - top)
        inverse = 1.0 / (
            own_part * stats[j, 1:2] + far_part * stats[j, 4:5]
            + jnp.sum(weight, axis=0, keepdims=True) + sink_weight
        )
        delta = inverse * (
            own_part * stats[j, 2:3] + far_part * stats[j, 5:6]
            + jnp.sum(weight * lift, axis=0, keepdims=True)
        )
        chance = weight * inverse
        ds_t = (chance * (lift - delta)).astype(bf16)
        dscore[j, 2 * length :] = ds_t
        stats[j, 0:1] = own_part * inverse
        stats[j, 3:4] = far_part * inverse
        stats[j, 6:7] = delta
        key_all = jnp.dot(ds_t, q_part, preferred_element_type=f32) * scale
        value_all = jnp.dot(chance.astype(bf16), g_part, preferred_element_type=f32)
        for i in range(ny):
            terms[j, i, :, :HDIM] = key_all[i * nx : (i + 1) * nx].astype(bf16)
            terms[j, i, :, HDIM:] = value_all[i * nx : (i + 1) * nx].astype(bf16)
        terms_in[j, y] = terms[j, y]
        for d in range(1, ny):
            t_copies.append(send(
                terms.at[j, (y + d) % ny], terms_in.at[j, y],
                t_send.at[j, d - 1], t_recv.at[j, d - 1], y_peer(d),
            ))
        sink_term = sink_weight * inverse * delta
        for h in range(GROUP):
            part = jnp.sum(sink_term[:, h * length : (h + 1) * length], axis=1, keepdims=True)
            sink_line = jnp.where(sink_lane == j * GROUP + h, part, sink_line)
    sink_buf[...] = sink_line
    sink_dp[pl.ds(dp, 1), :] = sink_line
    dp_copies = [
        send(sink_buf, sink_dp.at[pl.ds(dp, 1)], sd_send.at[d - 1], sd_recv.at[d - 1], dp_peer(d))
        for d in range(1, ndp)
    ]

    def gradients(which, j):
        chance = weights[j, which] * stats[j, 3 * which : 3 * which + 1]
        ds_t = (chance * (lifts[j, which] - stats[j, 6:7])).astype(bf16)
        dscore[j, which * length : (which + 1) * length] = ds_t
        key_part = jnp.dot(ds_t, heads_of(q_ref, j), preferred_element_type=f32) * scale
        value_part = jnp.dot(chance.astype(bf16), heads_of(g_ref, j), preferred_element_type=f32)
        return key_part, value_part

    back_copies = []
    for j in range(KV_HEADS):
        key_part, value_part = gradients(1, j)
        back_buf[j, :, :HDIM] = key_part.astype(bf16)
        back_buf[j, :, HDIM:] = value_part.astype(bf16)
        back_copies.append(send(
            back_buf.at[j], back.at[j], back_send.at[j], back_recv.at[j], partner
        ))

    def own_gradients(j):
        cut = slice(j * HDIM, (j + 1) * HDIM)
        own_k[:, cut], own_v[:, cut] = gradients(0, j)

    def query_gradients(j):
        low = j * HDIM
        keys = jnp.concatenate(
            [k_ref[:, low : low + HDIM], far_k[:, low : low + HDIM], panel_kv[:, low : low + HDIM]], 0
        )
        query_part = scale * lax.dot_general(
            dscore[j], keys, (((0,), (0,)), ((), ())), preferred_element_type=f32
        )
        for h in range(GROUP):
            first = (j * GROUP + h) * HDIM
            dq_ref[:, first : first + HDIM] = query_part[h * length : (h + 1) * length].astype(bf16)

    for j in range(KV_HEADS):
        own_gradients(j)
    arrived(dp_copies)
    sink_sum = jnp.sum(sink_dp[...], axis=0, keepdims=True)
    sink_part[...] = sink_sum
    sink_y[pl.ds(y, 1), :] = sink_sum
    sy_copies = [
        send(sink_part, sink_y.at[pl.ds(y, 1)], sy_send.at[d - 1], sy_recv.at[d - 1], y_peer(d))
        for d in range(1, ny)
    ]
    for j in range(KV_HEADS // 2):
        query_gradients(j)
    arrived(t_copies)
    for j in range(KV_HEADS):
        total = terms_in[j, 0].astype(f32)
        for i in range(1, ny):
            total = total + terms_in[j, i].astype(f32)
        lines[:, j * HDIM : (j + 1) * HDIM] = total[:, :HDIM]
        lines[:, WIDTH + j * HDIM : WIDTH + (j + 1) * HDIM] = total[:, HDIM:]
    lines_in[pl.ds(x, 1), :] = lines[pl.ds(x, 1), :]
    l_copies = [
        send(lines.at[pl.ds((x + d) % nx, 1)], lines_in.at[pl.ds(x, 1)],
             l_send.at[d - 1], l_recv.at[d - 1], x_peer(d))
        for d in range(1, nx)
    ]
    arrived(sy_copies)
    sink_sum = jnp.sum(sink_y[...], axis=0, keepdims=True)
    sink_last[...] = sink_sum
    sink_x[pl.ds(x, 1), :] = sink_sum
    sx_copies = [
        send(sink_last, sink_x.at[pl.ds(x, 1)], sx_send.at[d - 1], sx_recv.at[d - 1], x_peer(d))
        for d in range(1, nx)
    ]
    for j in range(KV_HEADS // 2, KV_HEADS):
        query_gradients(j)
    arrived(back_copies)
    arrived(l_copies)
    line = jnp.sum(lines_in[...], axis=0, keepdims=True)
    here = lax.broadcasted_iota(jnp.int32, (length, HDIM), 0) == picked
    for j in range(KV_HEADS):
        cut = slice(j * HDIM, (j + 1) * HDIM)
        dk_ref[:, cut] = (
            own_k[:, cut] + back[j, :, :HDIM].astype(f32) + jnp.where(here, line[:, cut], 0.0)
        ).astype(bf16)
        dv_ref[:, cut] = (
            own_v[:, cut]
            + back[j, :, HDIM:].astype(f32)
            + jnp.where(here, line[:, WIDTH + j * HDIM : WIDTH + (j + 1) * HDIM], 0.0)
        ).astype(bf16)
    arrived(sx_copies)
    ds_ref[...] = -jnp.sum(sink_x[...], axis=0, keepdims=True)
    for copy in started:
        copy.wait_send()


def store_kernel(dq_ref, dk_ref, dv_ref, ds_ref, dq_out, dk_out, dv_out, ds_out, out_sem):
    copies = [
        pltpu.make_async_copy(src, dst, out_sem.at[i])
        for i, (src, dst) in enumerate([(dq_ref, dq_out), (dk_ref, dk_out), (dv_ref, dv_out)])
    ]
    for copy in copies:
        copy.start()
    ds_out[...] = ds_ref[:, :HEADS]
    for copy in copies:
        copy.wait()


def on_device(
    ndp, query_rows, key_rows, value_rows, grad_rows, bucket_rank, sample_rows, sample_count, sink_logit
):
    length = query_rows.shape[1]
    slots = lax.axis_size("ctx")
    nx = 8 if slots >= 64 else 2
    ny = slots // nx
    keys = 2 * length + slots
    wide = GROUP * length
    f32, bf16, i32 = jnp.float32, jnp.bfloat16, jnp.int32
    vmem, smem, dma = pltpu.VMEM, pltpu.SMEM, pltpu.SemaphoreType.DMA
    space = pl.BlockSpec(memory_space=pltpu.VMEM)
    far = pl.BlockSpec(memory_space=pltpu.HBM)
    grads = [
        jax.ShapeDtypeStruct((length, HEADS * HDIM), bf16),
        jax.ShapeDtypeStruct((length, WIDTH), bf16),
        jax.ShapeDtypeStruct((length, WIDTH), bf16),
    ]
    results = pl.pallas_call(
        functools.partial(whole_kernel, ny, nx, ndp),
        out_shape=grads + [jax.ShapeDtypeStruct((1, 128), f32)],
        in_specs=[far] * 8,
        out_specs=[space] * 4,
        scratch_shapes=[
            vmem((length, HEADS * HDIM), bf16),
            vmem((length, WIDTH), bf16),
            vmem((length, WIDTH), bf16),
            vmem((length, HEADS * HDIM), bf16),
            vmem((1, length), i32),
            smem((1, 1), i32),
            smem((1, 1), i32),
            smem((HEADS,), f32),
            vmem((8, ROW), f32),
            vmem((nx, ROW), f32),
            vmem((nx, ROW), bf16),
            vmem((ny, nx, ROW), bf16),
            vmem((length, WIDTH), bf16),
            vmem((length, WIDTH), bf16),
            vmem((1, length), i32),
            vmem((KV_HEADS, 2, length, wide), f32),
            vmem((KV_HEADS, 2, length, wide), f32),
            vmem((KV_HEADS, 8, wide), f32),
            vmem((KV_HEADS, keys, wide), bf16),
            vmem((length, WIDTH), f32),
            vmem((length, WIDTH), f32),
            vmem((KV_HEADS, length, 2 * HDIM), bf16),
            vmem((KV_HEADS, length, 2 * HDIM), bf16),
            vmem((KV_HEADS, ny, nx, 2 * HDIM), bf16),
            vmem((KV_HEADS, ny, nx, 2 * HDIM), bf16),
            vmem((nx, 2 * WIDTH), f32),
            vmem((nx, 2 * WIDTH), f32),
            vmem((1, 128), f32),
            vmem((ndp, 128), f32),
            vmem((1, 128), f32),
            vmem((ny, 128), f32),
            vmem((1, 128), f32),
            vmem((nx, 128), f32),
            dma((8,)),
            dma((nx - 1,)), dma((nx - 1,)),
            dma((ny - 1,)), dma((ny - 1,)),
            dma((3,)), dma((3,)),
            dma((KV_HEADS,)), dma((KV_HEADS,)),
            dma((KV_HEADS, ny - 1)), dma((KV_HEADS, ny - 1)),
            dma((nx - 1,)), dma((nx - 1,)),
            dma((ndp - 1,)), dma((ndp - 1,)),
            dma((ny - 1,)), dma((ny - 1,)),
            dma((nx - 1,)), dma((nx - 1,)),
        ],
        compiler_params=pltpu.CompilerParams(
            collective_id=0, has_side_effects=True, vmem_limit_bytes=40 << 20
        ),
    )(
        query_rows[0], key_rows[0], value_rows[0], grad_rows[0],
        bucket_rank, sample_rows, sample_count, sink_logit,
    )
    dq, dk, dv, ds = pl.pallas_call(
        store_kernel,
        out_shape=grads + [jax.ShapeDtypeStruct((1, HEADS), f32)],
        in_specs=[space] * 4,
        out_specs=[far] * 3 + [space],
        scratch_shapes=[dma((3,))],
        compiler_params=pltpu.CompilerParams(vmem_limit_bytes=8 << 20),
    )(*results)
    return dq[None], dk[None], dv[None], ds[0]


def solution(mesh):
    return jax.shard_map(
        functools.partial(on_device, mesh.shape["dp"]),
        mesh=mesh,
        in_specs=(
            P("dp", "ctx", None),
            P("dp", "ctx", None),
            P("dp", "ctx", None),
            P("dp", "ctx", None),
            P("dp", "ctx"),
            P("dp", "ctx"),
            P("dp", "ctx"),
            P(),
        ),
        out_specs=(P("dp", "ctx", None), P("dp", "ctx", None), P("dp", "ctx", None), P()),
        check_vma=False,
    )
```

```python
import functools

import jax
import jax.numpy as jnp
from jax import lax
from jax.experimental import pallas as pl
from jax.experimental.pallas import tpu as pltpu
from jax.sharding import PartitionSpec as P

HEADS = 16
KV_HEADS = 4
HDIM = 128
BUCKET = 128
GROUP = HEADS // KV_HEADS
WIDTH = KV_HEADS * HDIM
ROW = 2 * WIDTH + 128
NEG = -1e30
EARLY = 1
MESH = pl.DeviceIdType.MESH


def whole_kernel(
    ny, nx, ndp,
    q_hbm, k_hbm, v_hbm, g_hbm, rank_hbm, rows_hbm, count_hbm, sink_hbm,
    dq_ref, dk_ref, dv_ref, ds_ref,
    q_ref, k_ref, v_ref, g_ref, rank_ref, rows_ref, count_ref, sink_ref,
    row_buf, rows1, blk_buf, samples, far_k, far_v, far_rank,
    weights, lifts, stats, dscore, sample_prob, own_k, own_v, back_buf, back,
    terms, terms_in, lines, lines_in,
    sink_buf, sink_dp, sink_part, sink_y, sink_last, sink_x,
    in_sem, x_send, x_recv, y_send, y_recv, pair_send, pair_recv,
    back_send, back_recv, t_send, t_recv, l_send, l_recv,
    sd_send, sd_recv, sy_send, sy_recv, sx_send, sx_recv,
):
    f32, bf16 = jnp.float32, jnp.bfloat16
    length = k_ref.shape[0]
    slots = ny * nx
    scale = HDIM ** (-0.5)
    ctx, dp = lax.axis_index("ctx"), lax.axis_index("dp")
    y, x = ctx // nx, ctx % nx

    def x_peer(d):
        return {"ctx": y * nx + (x + d) % nx}

    def y_peer(d):
        return {"ctx": ((y + d) % ny) * nx + x}

    def dp_peer(d):
        return {"dp": (dp + d) % ndp}

    partner = {"ctx": y * nx + x + 1 - 2 * (x % 2)}
    started = []

    def send(src, dst, ssem, rsem, device):
        copy = pltpu.make_async_remote_copy(
            src_ref=src, dst_ref=dst, send_sem=ssem, recv_sem=rsem,
            device_id=device, device_id_type=MESH,
        )
        copy.start()
        started.append(copy)
        return copy

    def arrived(copies):
        for copy in copies:
            copy.wait_recv()

    loads = [
        pltpu.make_async_copy(src, dst, in_sem.at[i])
        for i, (src, dst) in enumerate(
            [
                (rank_hbm, rank_ref), (rows_hbm, rows_ref), (count_hbm, count_ref),
                (k_hbm, k_ref), (v_hbm, v_ref), (sink_hbm, sink_ref),
                (q_hbm, q_ref), (g_hbm, g_ref),
            ]
        )
    ]
    for load in loads:
        load.start()
    barrier = pltpu.get_barrier_semaphore()
    peers = (
        [x_peer(d) for d in range(1, nx)]
        + [y_peer(d) for d in range(1, ny)]
        + [dp_peer(d) for d in range(1, ndp)]
    )
    for peer in peers:
        pl.semaphore_signal(barrier, inc=1, device_id=peer, device_id_type=MESH)
    for load in loads[:5]:
        load.wait()

    picked = rows_ref[0, 0]
    hit = lax.broadcasted_iota(jnp.int32, (8, length), 1) == picked
    one_hot = jnp.where(hit, 1.0, 0.0).astype(bf16)
    own_bucket = jnp.where(rank_ref[...] >= BUCKET, 1.0, 0.0)
    mark = jnp.sum(jnp.where(hit, own_bucket, 0.0), axis=1, keepdims=True)
    row_buf[:, :WIDTH] = jnp.dot(one_hot, k_ref[...], preferred_element_type=f32)
    row_buf[:, WIDTH : 2 * WIDTH] = jnp.dot(one_hot, v_ref[...], preferred_element_type=f32)
    tail = lax.broadcasted_iota(jnp.int32, (8, 128), 1)
    row_buf[:, 2 * WIDTH :] = jnp.where(
        tail == 0, count_ref[0, 0].astype(f32), jnp.where(tail == 1, mark, 0.0)
    )
    rows1[pl.ds(x, 1), :] = row_buf[0:1, :]
    pl.semaphore_wait(barrier, len(peers))

    x_copies = [
        send(row_buf.at[pl.ds(0, 1)], rows1.at[pl.ds(x, 1)],
             x_send.at[d - 1], x_recv.at[d - 1], x_peer(d))
        for d in range(1, nx)
    ]
    pair_copies = [
        send(rank_ref, far_rank, pair_send.at[0], pair_recv.at[0], partner),
        send(k_ref, far_k, pair_send.at[1], pair_recv.at[1], partner),
        send(v_ref, far_v, pair_send.at[2], pair_recv.at[2], partner),
    ]
    for load in loads[5:]:
        load.wait()

    up = lax.broadcasted_iota(jnp.int32, (length, length), 0)
    across = lax.broadcasted_iota(jnp.int32, (length, length), 1)

    def inside(line):
        upright = jnp.sum(jnp.where(up == across, line, 0.0), axis=1, keepdims=True)
        return jnp.concatenate([jnp.where(upright == own_bucket, 0.0, NEG)] * GROUP, 1)

    def heads_of(ref, j):
        first = j * GROUP * HDIM
        return jnp.concatenate(
            [ref[:, first + h * HDIM : first + (h + 1) * HDIM] for h in range(GROUP)], 0
        )

    def across_dot(left, right):
        return lax.dot_general(
            left, right, (((1,), (1,)), ((), ())), preferred_element_type=f32
        )

    def sink_of(j):
        return jnp.concatenate(
            [jnp.full((1, length), sink_ref[j * GROUP + h], f32) for h in range(GROUP)], 1
        )

    def score_block(which, keys, values, bias, j):
        cut = slice(j * HDIM, (j + 1) * HDIM)
        score = across_dot(keys[:, cut], heads_of(q_ref, j)) * scale + bias
        lift = across_dot(values[:, cut], heads_of(g_ref, j))
        top = jnp.max(score, axis=0, keepdims=True)
        weight = jnp.exp(score - top)
        weights[j, which] = weight
        lifts[j, which] = lift
        stats[j, 3 * which : 3 * which + 1] = top
        stats[j, 3 * which + 1 : 3 * which + 2] = jnp.sum(weight, axis=0, keepdims=True)
        stats[j, 3 * which + 2 : 3 * which + 3] = jnp.sum(weight * lift, axis=0, keepdims=True)

    own_bias = inside(own_bucket)
    for j in range(EARLY):
        score_block(0, k_ref, v_ref, own_bias, j)
    arrived(x_copies)
    blk_buf[...] = rows1[...].astype(bf16)
    samples[y] = rows1[...].astype(bf16)
    y_copies = [
        send(blk_buf, samples.at[y], y_send.at[d - 1], y_recv.at[d - 1], y_peer(d))
        for d in range(1, ny)
    ]
    for j in range(EARLY, KV_HEADS):
        score_block(0, k_ref, v_ref, own_bias, j)
    arrived(pair_copies)
    far_bias = inside(jnp.where(far_rank[...] >= BUCKET, 1.0, 0.0))
    for j in range(KV_HEADS):
        score_block(1, far_k, far_v, far_bias, j)
    arrived(y_copies)

    panel = jnp.concatenate([samples[i].astype(f32) for i in range(ny)], 0)
    panel_kv = panel[:, : 2 * WIDTH].astype(bf16)
    counts = panel[:, 2 * WIDTH : 2 * WIDTH + 1]
    marks = panel[:, 2 * WIDTH + 1 : 2 * WIDTH + 2]
    slot = lax.broadcasted_iota(jnp.int32, (slots, 1), 0)
    near = jnp.where(slot // 2 == ctx // 2, marks, 2.0)
    bias = jnp.concatenate([jnp.where(near == own_bucket, NEG, jnp.log(counts))] * GROUP, 1)
    sink_lane = lax.broadcasted_iota(jnp.int32, (1, 128), 1)
    sink_line = jnp.zeros((1, 128), f32)
    for j in range(KV_HEADS):
        low = j * HDIM
        q_part, g_part = heads_of(q_ref, j), heads_of(g_ref, j)
        score = across_dot(panel_kv[:, low : low + HDIM], q_part) * scale + bias
        lift = across_dot(panel_kv[:, WIDTH + low : WIDTH + low + HDIM], g_part)
        sink_row = sink_of(j)
        own_top, far_top = stats[j, 0:1], stats[j, 3:4]
        top = jnp.maximum(
            jnp.maximum(own_top, far_top),
            jnp.maximum(jnp.max(score, axis=0, keepdims=True), sink_row),
        )
        weight = jnp.exp(score - top)
        own_part, far_part = jnp.exp(own_top - top), jnp.exp(far_top - top)
        sink_weight = jnp.exp(sink_row - top)
        inverse = 1.0 / (
            own_part * stats[j, 1:2] + far_part * stats[j, 4:5]
            + jnp.sum(weight, axis=0, keepdims=True) + sink_weight
        )
        delta = inverse * (
            own_part * stats[j, 2:3] + far_part * stats[j, 5:6]
            + jnp.sum(weight * lift, axis=0, keepdims=True)
        )
        chance = weight * inverse
        ds_t = (chance * (lift - delta)).astype(bf16)
        dscore[j, 2 * length :] = ds_t
        stats[j, 0:1] = own_part * inverse
        stats[j, 3:4] = far_part * inverse
        stats[j, 6:7] = delta
        sample_prob[j] = chance.astype(bf16)
        sink_term = sink_weight * inverse * delta
        for h in range(GROUP):
            part = jnp.sum(sink_term[:, h * length : (h + 1) * length], axis=1, keepdims=True)
            sink_line = jnp.where(sink_lane == j * GROUP + h, part, sink_line)
    sink_buf[...] = sink_line
    sink_dp[pl.ds(dp, 1), :] = sink_line
    dp_copies = [
        send(sink_buf, sink_dp.at[pl.ds(dp, 1)], sd_send.at[d - 1], sd_recv.at[d - 1], dp_peer(d))
        for d in range(1, ndp)
    ]

    t_copies = []
    for j in range(KV_HEADS):
        key_all = jnp.dot(
            dscore[j, 2 * length :], heads_of(q_ref, j), preferred_element_type=f32) * scale
        value_all = jnp.dot(
            sample_prob[j], heads_of(g_ref, j), preferred_element_type=f32)
        for i in range(ny):
            terms[j, i, :, :HDIM] = key_all[i * nx : (i + 1) * nx].astype(bf16)
            terms[j, i, :, HDIM:] = value_all[i * nx : (i + 1) * nx].astype(bf16)
        terms_in[j, y] = terms[j, y]
        for d in range(1, ny):
            t_copies.append(send(
                terms.at[j, (y + d) % ny], terms_in.at[j, y],
                t_send.at[j, d - 1], t_recv.at[j, d - 1], y_peer(d),
            ))

    def gradients(which, j):
        chance = weights[j, which] * stats[j, 3 * which : 3 * which + 1]
        ds_t = (chance * (lifts[j, which] - stats[j, 6:7])).astype(bf16)
        dscore[j, which * length : (which + 1) * length] = ds_t
        key_part = jnp.dot(ds_t, heads_of(q_ref, j), preferred_element_type=f32) * scale
        value_part = jnp.dot(chance.astype(bf16), heads_of(g_ref, j), preferred_element_type=f32)
        return key_part, value_part

    back_copies = []
    for j in range(KV_HEADS):
        key_part, value_part = gradients(1, j)
        back_buf[j, :, :HDIM] = key_part.astype(bf16)
        back_buf[j, :, HDIM:] = value_part.astype(bf16)
        back_copies.append(send(
            back_buf.at[j], back.at[j], back_send.at[j], back_recv.at[j], partner
        ))

    def own_gradients(j):
        cut = slice(j * HDIM, (j + 1) * HDIM)
        own_k[:, cut], own_v[:, cut] = gradients(0, j)

    def query_gradients(j):
        low = j * HDIM
        keys = jnp.concatenate(
            [k_ref[:, low : low + HDIM], far_k[:, low : low + HDIM], panel_kv[:, low : low + HDIM]], 0
        )
        query_part = scale * lax.dot_general(
            dscore[j], keys, (((0,), (0,)), ((), ())), preferred_element_type=f32
        )
        for h in range(GROUP):
            first = (j * GROUP + h) * HDIM
            dq_ref[:, first : first + HDIM] = query_part[h * length : (h + 1) * length].astype(bf16)

    arrived(dp_copies)
    sink_sum = jnp.sum(sink_dp[...], axis=0, keepdims=True)
    sink_part[...] = sink_sum
    sink_y[pl.ds(y, 1), :] = sink_sum
    sy_copies = [
        send(sink_part, sink_y.at[pl.ds(y, 1)], sy_send.at[d - 1], sy_recv.at[d - 1], y_peer(d))
        for d in range(1, ny)
    ]
    for j in range(KV_HEADS):
        own_gradients(j)
    arrived(t_copies)
    for j in range(KV_HEADS):
        total = terms_in[j, 0].astype(f32)
        for i in range(1, ny):
            total = total + terms_in[j, i].astype(f32)
        lines[:, j * HDIM : (j + 1) * HDIM] = total[:, :HDIM]
        lines[:, WIDTH + j * HDIM : WIDTH + (j + 1) * HDIM] = total[:, HDIM:]
    lines_in[pl.ds(x, 1), :] = lines[pl.ds(x, 1), :]
    l_copies = [
        send(lines.at[pl.ds((x + d) % nx, 1)], lines_in.at[pl.ds(x, 1)],
             l_send.at[d - 1], l_recv.at[d - 1], x_peer(d))
        for d in range(1, nx)
    ]
    arrived(sy_copies)
    sink_sum = jnp.sum(sink_y[...], axis=0, keepdims=True)
    sink_last[...] = sink_sum
    sink_x[pl.ds(x, 1), :] = sink_sum
    sx_copies = [
        send(sink_last, sink_x.at[pl.ds(x, 1)], sx_send.at[d - 1], sx_recv.at[d - 1], x_peer(d))
        for d in range(1, nx)
    ]
    for j in range(KV_HEADS):
        query_gradients(j)
    arrived(back_copies)
    arrived(l_copies)
    line = jnp.sum(lines_in[...], axis=0, keepdims=True)
    here = lax.broadcasted_iota(jnp.int32, (length, HDIM), 0) == picked
    for j in range(KV_HEADS):
        cut = slice(j * HDIM, (j + 1) * HDIM)
        dk_ref[:, cut] = (
            own_k[:, cut] + back[j, :, :HDIM].astype(f32) + jnp.where(here, line[:, cut], 0.0)
        ).astype(bf16)
        dv_ref[:, cut] = (
            own_v[:, cut]
            + back[j, :, HDIM:].astype(f32)
            + jnp.where(here, line[:, WIDTH + j * HDIM : WIDTH + (j + 1) * HDIM], 0.0)
        ).astype(bf16)
    arrived(sx_copies)
    ds_ref[...] = -jnp.sum(sink_x[...], axis=0, keepdims=True)
    for copy in started:
        copy.wait_send()


def store_kernel(dq_ref, dk_ref, dv_ref, ds_ref, dq_out, dk_out, dv_out, ds_out, out_sem):
    copies = [
        pltpu.make_async_copy(src, dst, out_sem.at[i])
        for i, (src, dst) in enumerate([(dq_ref, dq_out), (dk_ref, dk_out), (dv_ref, dv_out)])
    ]
    for copy in copies:
        copy.start()
    ds_out[...] = ds_ref[:, :HEADS]
    for copy in copies:
        copy.wait()


def on_device(
    ndp, query_rows, key_rows, value_rows, grad_rows, bucket_rank, sample_rows, sample_count, sink_logit
):
    length = query_rows.shape[1]
    slots = lax.axis_size("ctx")
    nx = 8 if slots >= 64 else 2
    ny = slots // nx
    keys = 2 * length + slots
    wide = GROUP * length
    f32, bf16, i32 = jnp.float32, jnp.bfloat16, jnp.int32
    vmem, smem, dma = pltpu.VMEM, pltpu.SMEM, pltpu.SemaphoreType.DMA
    space = pl.BlockSpec(memory_space=pltpu.VMEM)
    far = pl.BlockSpec(memory_space=pltpu.HBM)
    grads = [
        jax.ShapeDtypeStruct((length, HEADS * HDIM), bf16),
        jax.ShapeDtypeStruct((length, WIDTH), bf16),
        jax.ShapeDtypeStruct((length, WIDTH), bf16),
    ]
    results = pl.pallas_call(
        functools.partial(whole_kernel, ny, nx, ndp),
        out_shape=grads + [jax.ShapeDtypeStruct((1, 128), f32)],
        in_specs=[far] * 8,
        out_specs=[space] * 4,
        scratch_shapes=[
            vmem((length, HEADS * HDIM), bf16),
            vmem((length, WIDTH), bf16),
            vmem((length, WIDTH), bf16),
            vmem((length, HEADS * HDIM), bf16),
            vmem((1, length), i32),
            smem((1, 1), i32),
            smem((1, 1), i32),
            smem((HEADS,), f32),
            vmem((8, ROW), f32),
            vmem((nx, ROW), f32),
            vmem((nx, ROW), bf16),
            vmem((ny, nx, ROW), bf16),
            vmem((length, WIDTH), bf16),
            vmem((length, WIDTH), bf16),
            vmem((1, length), i32),
            vmem((KV_HEADS, 2, length, wide), f32),
            vmem((KV_HEADS, 2, length, wide), f32),
            vmem((KV_HEADS, 8, wide), f32),
            vmem((KV_HEADS, keys, wide), bf16),
            vmem((KV_HEADS, slots, wide), bf16),
            vmem((length, WIDTH), f32),
            vmem((length, WIDTH), f32),
            vmem((KV_HEADS, length, 2 * HDIM), bf16),
            vmem((KV_HEADS, length, 2 * HDIM), bf16),
            vmem((KV_HEADS, ny, nx, 2 * HDIM), bf16),
            vmem((KV_HEADS, ny, nx, 2 * HDIM), bf16),
            vmem((nx, 2 * WIDTH), f32),
            vmem((nx, 2 * WIDTH), f32),
            vmem((1, 128), f32),
            vmem((ndp, 128), f32),
            vmem((1, 128), f32),
            vmem((ny, 128), f32),
            vmem((1, 128), f32),
            vmem((nx, 128), f32),
            dma((8,)),
            dma((nx - 1,)), dma((nx - 1,)),
            dma((ny - 1,)), dma((ny - 1,)),
            dma((3,)), dma((3,)),
            dma((KV_HEADS,)), dma((KV_HEADS,)),
            dma((KV_HEADS, ny - 1)), dma((KV_HEADS, ny - 1)),
            dma((nx - 1,)), dma((nx - 1,)),
            dma((ndp - 1,)), dma((ndp - 1,)),
            dma((ny - 1,)), dma((ny - 1,)),
            dma((nx - 1,)), dma((nx - 1,)),
        ],
        compiler_params=pltpu.CompilerParams(
            collective_id=0, has_side_effects=True, vmem_limit_bytes=40 << 20
        ),
    )(
        *[
            pltpu.with_memory_space_constraint(array, pltpu.HBM)
            for array in (
                query_rows[0], key_rows[0], value_rows[0], grad_rows[0], bucket_rank
            )
        ],
        sample_rows, sample_count,
        pltpu.with_memory_space_constraint(sink_logit, pltpu.HBM),
    )
    dq, dk, dv, ds = pl.pallas_call(
        store_kernel,
        out_shape=grads + [jax.ShapeDtypeStruct((1, HEADS), f32)],
        in_specs=[space] * 4,
        out_specs=[far] * 3 + [space],
        scratch_shapes=[dma((3,))],
        compiler_params=pltpu.CompilerParams(vmem_limit_bytes=8 << 20),
    )(*results)
    return dq[None], dk[None], dv[None], ds[0]


def solution(mesh):
    return jax.shard_map(
        functools.partial(on_device, mesh.shape["dp"]),
        mesh=mesh,
        in_specs=(
            P("dp", "ctx", None),
            P("dp", "ctx", None),
            P("dp", "ctx", None),
            P("dp", "ctx", None),
            P("dp", "ctx"),
            P("dp", "ctx"),
            P("dp", "ctx"),
            P(),
        ),
        out_specs=(P("dp", "ctx", None), P("dp", "ctx", None), P("dp", "ctx", None), P()),
        check_vma=False,
    )
```

```python
import functools

import jax
import jax.numpy as jnp
from jax import lax
from jax.experimental import pallas as pl
from jax.experimental.pallas import tpu as pltpu
from jax.sharding import PartitionSpec as P

HEADS = 16
KV_HEADS = 4
HDIM = 128
BUCKET = 128
GROUP = HEADS // KV_HEADS
WIDTH = KV_HEADS * HDIM
ROW = 2 * WIDTH + 128
NEG = -1e30
EARLY = 1
FAR_FIRST = 2
MESH = pl.DeviceIdType.MESH


def whole_kernel(
    ny, nx, ndp,
    q_hbm, k_hbm, v_hbm, g_hbm, rank_hbm, rows_hbm, count_hbm, sink_hbm,
    dq_ref, dk_ref, dv_ref, ds_ref,
    q_ref, k_ref, v_ref, g_ref, rank_ref, rows_ref, count_ref, sink_ref,
    row_buf, rows1, blk_buf, samples, far_k, far_v, far_rank,
    weights, lifts, stats, dscore, sample_prob, own_k, own_v, back_buf, back,
    terms, terms_in, lines, lines_in,
    sink_buf, sink_dp, sink_part, sink_y, sink_last, sink_x,
    in_sem, x_send, x_recv, y_send, y_recv, pair_send, pair_recv,
    back_send, back_recv, t_send, t_recv, l_send, l_recv,
    sd_send, sd_recv, sy_send, sy_recv, sx_send, sx_recv,
):
    f32, bf16 = jnp.float32, jnp.bfloat16
    length = k_ref.shape[0]
    slots = ny * nx
    scale = HDIM ** (-0.5)
    ctx, dp = lax.axis_index("ctx"), lax.axis_index("dp")
    y, x = ctx // nx, ctx % nx

    def x_peer(d):
        return {"ctx": y * nx + (x + d) % nx}

    def y_peer(d):
        return {"ctx": ((y + d) % ny) * nx + x}

    def dp_peer(d):
        return {"dp": (dp + d) % ndp}

    partner = {"ctx": y * nx + x + 1 - 2 * (x % 2)}
    started = []

    def send(src, dst, ssem, rsem, device):
        copy = pltpu.make_async_remote_copy(
            src_ref=src, dst_ref=dst, send_sem=ssem, recv_sem=rsem,
            device_id=device, device_id_type=MESH,
        )
        copy.start()
        started.append(copy)
        return copy

    def arrived(copies):
        for copy in copies:
            copy.wait_recv()

    loads = [
        pltpu.make_async_copy(src, dst, in_sem.at[i])
        for i, (src, dst) in enumerate(
            [
                (rank_hbm, rank_ref), (rows_hbm, rows_ref), (count_hbm, count_ref),
                (k_hbm, k_ref), (v_hbm, v_ref), (sink_hbm, sink_ref),
                (q_hbm, q_ref), (g_hbm, g_ref),
            ]
        )
    ]
    for load in loads:
        load.start()
    barrier = pltpu.get_barrier_semaphore()
    def outward(size):
        return sorted(range(1, size), key=lambda d: -min(d, size - d))

    peers = (
        [x_peer(d) for d in outward(nx)]
        + [y_peer(d) for d in outward(ny)]
        + [dp_peer(d) for d in outward(ndp)]
    )
    for peer in peers:
        pl.semaphore_signal(barrier, inc=1, device_id=peer, device_id_type=MESH)
    for load in loads[:5]:
        load.wait()

    picked = rows_ref[0, 0]
    hit = lax.broadcasted_iota(jnp.int32, (8, length), 1) == picked
    one_hot = jnp.where(hit, 1.0, 0.0).astype(bf16)
    own_bucket = jnp.where(rank_ref[...] >= BUCKET, 1.0, 0.0)
    mark = jnp.sum(jnp.where(hit, own_bucket, 0.0), axis=1, keepdims=True)
    row_buf[:, :WIDTH] = jnp.dot(one_hot, k_ref[...], preferred_element_type=f32)
    row_buf[:, WIDTH : 2 * WIDTH] = jnp.dot(one_hot, v_ref[...], preferred_element_type=f32)
    tail = lax.broadcasted_iota(jnp.int32, (8, 128), 1)
    row_buf[:, 2 * WIDTH :] = jnp.where(
        tail == 0, count_ref[0, 0].astype(f32), jnp.where(tail == 1, mark, 0.0)
    )
    rows1[pl.ds(x, 1), :] = row_buf[0:1, :]
    pl.semaphore_wait(barrier, len(peers))

    x_copies = [
        send(row_buf.at[pl.ds(0, 1)], rows1.at[pl.ds(x, 1)],
             x_send.at[d - 1], x_recv.at[d - 1], x_peer(d))
        for d in outward(nx)
    ]
    pair_copies = [
        send(rank_ref, far_rank, pair_send.at[0], pair_recv.at[0], partner),
        send(k_ref, far_k, pair_send.at[1], pair_recv.at[1], partner),
        send(v_ref, far_v, pair_send.at[2], pair_recv.at[2], partner),
    ]
    for load in loads[5:]:
        load.wait()

    up = lax.broadcasted_iota(jnp.int32, (length, length), 0)
    across = lax.broadcasted_iota(jnp.int32, (length, length), 1)

    def inside(line):
        upright = jnp.sum(jnp.where(up == across, line, 0.0), axis=1, keepdims=True)
        return jnp.concatenate([jnp.where(upright == own_bucket, 0.0, NEG)] * GROUP, 1)

    def heads_of(ref, j):
        first = j * GROUP * HDIM
        return jnp.concatenate(
            [ref[:, first + h * HDIM : first + (h + 1) * HDIM] for h in range(GROUP)], 0
        )

    def across_dot(left, right):
        return lax.dot_general(
            left, right, (((1,), (1,)), ((), ())), preferred_element_type=f32
        )

    def sink_of(j):
        return jnp.concatenate(
            [jnp.full((1, length), sink_ref[j * GROUP + h], f32) for h in range(GROUP)], 1
        )

    def score_block(which, keys, values, bias, j):
        cut = slice(j * HDIM, (j + 1) * HDIM)
        score = across_dot(keys[:, cut], heads_of(q_ref, j)) * scale + bias
        lift = across_dot(values[:, cut], heads_of(g_ref, j))
        top = jnp.max(score, axis=0, keepdims=True)
        weight = jnp.exp(score - top)
        weights[j, which] = weight
        lifts[j, which] = lift
        stats[j, 3 * which : 3 * which + 1] = top
        stats[j, 3 * which + 1 : 3 * which + 2] = jnp.sum(weight, axis=0, keepdims=True)
        stats[j, 3 * which + 2 : 3 * which + 3] = jnp.sum(weight * lift, axis=0, keepdims=True)

    own_bias = inside(own_bucket)
    for j in range(EARLY):
        score_block(0, k_ref, v_ref, own_bias, j)
    arrived(x_copies)
    blk_buf[...] = rows1[...].astype(bf16)
    samples[y] = rows1[...].astype(bf16)
    y_copies = [
        send(blk_buf, samples.at[y], y_send.at[d - 1], y_recv.at[d - 1], y_peer(d))
        for d in outward(ny)
    ]
    for j in range(EARLY, KV_HEADS):
        score_block(0, k_ref, v_ref, own_bias, j)
    arrived(pair_copies)
    far_bias = inside(jnp.where(far_rank[...] >= BUCKET, 1.0, 0.0))
    for j in range(KV_HEADS):
        score_block(1, far_k, far_v, far_bias, j)
    arrived(y_copies)

    panel = jnp.concatenate([samples[i].astype(f32) for i in range(ny)], 0)
    panel_kv = panel[:, : 2 * WIDTH].astype(bf16)
    counts = panel[:, 2 * WIDTH : 2 * WIDTH + 1]
    marks = panel[:, 2 * WIDTH + 1 : 2 * WIDTH + 2]
    slot = lax.broadcasted_iota(jnp.int32, (slots, 1), 0)
    near = jnp.where(slot // 2 == ctx // 2, marks, 2.0)
    bias = jnp.concatenate([jnp.where(near == own_bucket, NEG, jnp.log(counts))] * GROUP, 1)
    sink_lane = lax.broadcasted_iota(jnp.int32, (1, 128), 1)
    sink_line = jnp.zeros((1, 128), f32)
    for j in range(KV_HEADS):
        low = j * HDIM
        q_part, g_part = heads_of(q_ref, j), heads_of(g_ref, j)
        score = across_dot(panel_kv[:, low : low + HDIM], q_part) * scale + bias
        lift = across_dot(panel_kv[:, WIDTH + low : WIDTH + low + HDIM], g_part)
        sink_row = sink_of(j)
        own_top, far_top = stats[j, 0:1], stats[j, 3:4]
        top = jnp.maximum(
            jnp.maximum(own_top, far_top),
            jnp.maximum(jnp.max(score, axis=0, keepdims=True), sink_row),
        )
        weight = jnp.exp(score - top)
        own_part, far_part = jnp.exp(own_top - top), jnp.exp(far_top - top)
        sink_weight = jnp.exp(sink_row - top)
        inverse = 1.0 / (
            own_part * stats[j, 1:2] + far_part * stats[j, 4:5]
            + jnp.sum(weight, axis=0, keepdims=True) + sink_weight
        )
        delta = inverse * (
            own_part * stats[j, 2:3] + far_part * stats[j, 5:6]
            + jnp.sum(weight * lift, axis=0, keepdims=True)
        )
        chance = weight * inverse
        ds_t = (chance * (lift - delta)).astype(bf16)
        dscore[j, 2 * length :] = ds_t
        stats[j, 0:1] = own_part * inverse
        stats[j, 3:4] = far_part * inverse
        stats[j, 6:7] = delta
        sample_prob[j] = chance.astype(bf16)
        sink_term = sink_weight * inverse * delta
        for h in range(GROUP):
            part = jnp.sum(sink_term[:, h * length : (h + 1) * length], axis=1, keepdims=True)
            sink_line = jnp.where(sink_lane == j * GROUP + h, part, sink_line)
    sink_buf[...] = sink_line
    sink_dp[pl.ds(dp, 1), :] = sink_line
    dp_copies = [
        send(sink_buf, sink_dp.at[pl.ds(dp, 1)], sd_send.at[d - 1], sd_recv.at[d - 1], dp_peer(d))
        for d in outward(ndp)
    ]

    for j in range(KV_HEADS):
        key_all = jnp.dot(
            dscore[j, 2 * length :], heads_of(q_ref, j), preferred_element_type=f32) * scale
        value_all = jnp.dot(
            sample_prob[j], heads_of(g_ref, j), preferred_element_type=f32)
        for i in range(ny):
            terms[i, j, :, :HDIM] = key_all[i * nx : (i + 1) * nx].astype(bf16)
            terms[i, j, :, HDIM:] = value_all[i * nx : (i + 1) * nx].astype(bf16)
    terms_in[y] = terms[y]
    t_copies = [
        send(terms.at[(y + d) % ny], terms_in.at[y],
             t_send.at[d - 1], t_recv.at[d - 1], y_peer(d))
        for d in outward(ny)
    ]

    def gradients(which, j):
        chance = weights[j, which] * stats[j, 3 * which : 3 * which + 1]
        ds_t = (chance * (lifts[j, which] - stats[j, 6:7])).astype(bf16)
        dscore[j, which * length : (which + 1) * length] = ds_t
        key_part = jnp.dot(ds_t, heads_of(q_ref, j), preferred_element_type=f32) * scale
        value_part = jnp.dot(chance.astype(bf16), heads_of(g_ref, j), preferred_element_type=f32)
        return key_part, value_part

    back_copies = []
    def far_gradients(j):
        key_part, value_part = gradients(1, j)
        back_buf[j, :, :HDIM] = key_part.astype(bf16)
        back_buf[j, :, HDIM:] = value_part.astype(bf16)
        back_copies.append(send(
            back_buf.at[j], back.at[j], back_send.at[j], back_recv.at[j], partner
        ))

    def own_gradients(j):
        cut = slice(j * HDIM, (j + 1) * HDIM)
        own_k[:, cut], own_v[:, cut] = gradients(0, j)

    def query_gradients(j):
        low = j * HDIM
        keys = jnp.concatenate(
            [k_ref[:, low : low + HDIM], far_k[:, low : low + HDIM], panel_kv[:, low : low + HDIM]], 0
        )
        query_part = scale * lax.dot_general(
            dscore[j], keys, (((0,), (0,)), ((), ())), preferred_element_type=f32
        )
        for h in range(GROUP):
            first = (j * GROUP + h) * HDIM
            dq_ref[:, first : first + HDIM] = query_part[h * length : (h + 1) * length].astype(bf16)

    for j in range(FAR_FIRST):
        far_gradients(j)
    arrived(dp_copies)
    sink_sum = jnp.sum(sink_dp[...], axis=0, keepdims=True)
    sink_part[...] = sink_sum
    sink_y[pl.ds(y, 1), :] = sink_sum
    sy_copies = [
        send(sink_part, sink_y.at[pl.ds(y, 1)], sy_send.at[d - 1], sy_recv.at[d - 1], y_peer(d))
        for d in outward(ny)
    ]
    for j in range(FAR_FIRST, KV_HEADS):
        far_gradients(j)
    for j in range(KV_HEADS):
        own_gradients(j)
    arrived(t_copies)
    for j in range(KV_HEADS):
        total = terms_in[0, j].astype(f32)
        for i in range(1, ny):
            total = total + terms_in[i, j].astype(f32)
        lines[:, j * HDIM : (j + 1) * HDIM] = total[:, :HDIM]
        lines[:, WIDTH + j * HDIM : WIDTH + (j + 1) * HDIM] = total[:, HDIM:]
    lines_in[pl.ds(x, 1), :] = lines[pl.ds(x, 1), :]
    l_copies = [
        send(lines.at[pl.ds((x + d) % nx, 1)], lines_in.at[pl.ds(x, 1)],
             l_send.at[d - 1], l_recv.at[d - 1], x_peer(d))
        for d in outward(nx)
    ]
    arrived(sy_copies)
    sink_sum = jnp.sum(sink_y[...], axis=0, keepdims=True)
    sink_last[...] = sink_sum
    sink_x[pl.ds(x, 1), :] = sink_sum
    sx_copies = [
        send(sink_last, sink_x.at[pl.ds(x, 1)], sx_send.at[d - 1], sx_recv.at[d - 1], x_peer(d))
        for d in outward(nx)
    ]
    for j in range(KV_HEADS):
        query_gradients(j)
    arrived(back_copies)
    arrived(l_copies)
    line = jnp.sum(lines_in[...], axis=0, keepdims=True)
    here = lax.broadcasted_iota(jnp.int32, (length, HDIM), 0) == picked
    for j in range(KV_HEADS):
        cut = slice(j * HDIM, (j + 1) * HDIM)
        dk_ref[:, cut] = (
            own_k[:, cut] + back[j, :, :HDIM].astype(f32) + jnp.where(here, line[:, cut], 0.0)
        ).astype(bf16)
        dv_ref[:, cut] = (
            own_v[:, cut]
            + back[j, :, HDIM:].astype(f32)
            + jnp.where(here, line[:, WIDTH + j * HDIM : WIDTH + (j + 1) * HDIM], 0.0)
        ).astype(bf16)
    arrived(sx_copies)
    ds_ref[...] = -jnp.sum(sink_x[...], axis=0, keepdims=True)
    for copy in started:
        copy.wait_send()


def store_kernel(dq_ref, dk_ref, dv_ref, ds_ref, dq_out, dk_out, dv_out, ds_out, out_sem):
    copies = [
        pltpu.make_async_copy(src, dst, out_sem.at[i])
        for i, (src, dst) in enumerate([(dq_ref, dq_out), (dk_ref, dk_out), (dv_ref, dv_out)])
    ]
    for copy in copies:
        copy.start()
    ds_out[...] = ds_ref[:, :HEADS]
    for copy in copies:
        copy.wait()


def on_device(
    ndp, query_rows, key_rows, value_rows, grad_rows, bucket_rank, sample_rows, sample_count, sink_logit
):
    length = query_rows.shape[1]
    slots = lax.axis_size("ctx")
    nx = 8 if slots >= 64 else 2
    ny = slots // nx
    keys = 2 * length + slots
    wide = GROUP * length
    f32, bf16, i32 = jnp.float32, jnp.bfloat16, jnp.int32
    vmem, smem, dma = pltpu.VMEM, pltpu.SMEM, pltpu.SemaphoreType.DMA
    space = pl.BlockSpec(memory_space=pltpu.VMEM)
    far = pl.BlockSpec(memory_space=pltpu.HBM)
    grads = [
        jax.ShapeDtypeStruct((length, HEADS * HDIM), bf16),
        jax.ShapeDtypeStruct((length, WIDTH), bf16),
        jax.ShapeDtypeStruct((length, WIDTH), bf16),
    ]
    results = pl.pallas_call(
        functools.partial(whole_kernel, ny, nx, ndp),
        out_shape=grads + [jax.ShapeDtypeStruct((1, 128), f32)],
        in_specs=[far] * 8,
        out_specs=[space] * 4,
        scratch_shapes=[
            vmem((length, HEADS * HDIM), bf16),
            vmem((length, WIDTH), bf16),
            vmem((length, WIDTH), bf16),
            vmem((length, HEADS * HDIM), bf16),
            vmem((1, length), i32),
            smem((1, 1), i32),
            smem((1, 1), i32),
            smem((HEADS,), f32),
            vmem((8, ROW), f32),
            vmem((nx, ROW), f32),
            vmem((nx, ROW), bf16),
            vmem((ny, nx, ROW), bf16),
            vmem((length, WIDTH), bf16),
            vmem((length, WIDTH), bf16),
            vmem((1, length), i32),
            vmem((KV_HEADS, 2, length, wide), f32),
            vmem((KV_HEADS, 2, length, wide), f32),
            vmem((KV_HEADS, 8, wide), f32),
            vmem((KV_HEADS, keys, wide), bf16),
            vmem((KV_HEADS, slots, wide), bf16),
            vmem((length, WIDTH), f32),
            vmem((length, WIDTH), f32),
            vmem((KV_HEADS, length, 2 * HDIM), bf16),
            vmem((KV_HEADS, length, 2 * HDIM), bf16),
            vmem((ny, KV_HEADS, nx, 2 * HDIM), bf16),
            vmem((ny, KV_HEADS, nx, 2 * HDIM), bf16),
            vmem((nx, 2 * WIDTH), f32),
            vmem((nx, 2 * WIDTH), f32),
            vmem((1, 128), f32),
            vmem((ndp, 128), f32),
            vmem((1, 128), f32),
            vmem((ny, 128), f32),
            vmem((1, 128), f32),
            vmem((nx, 128), f32),
            dma((8,)),
            dma((nx - 1,)), dma((nx - 1,)),
            dma((ny - 1,)), dma((ny - 1,)),
            dma((3,)), dma((3,)),
            dma((KV_HEADS,)), dma((KV_HEADS,)),
            dma((ny - 1,)), dma((ny - 1,)),
            dma((nx - 1,)), dma((nx - 1,)),
            dma((ndp - 1,)), dma((ndp - 1,)),
            dma((ny - 1,)), dma((ny - 1,)),
            dma((nx - 1,)), dma((nx - 1,)),
        ],
        compiler_params=pltpu.CompilerParams(
            collective_id=0, has_side_effects=True, vmem_limit_bytes=40 << 20
        ),
    )(
        *[
            pltpu.with_memory_space_constraint(array, pltpu.HBM)
            for array in (
                query_rows[0], key_rows[0], value_rows[0], grad_rows[0], bucket_rank
            )
        ],
        sample_rows, sample_count,
        pltpu.with_memory_space_constraint(sink_logit, pltpu.HBM),
    )
    dq, dk, dv, ds = pl.pallas_call(
        store_kernel,
        out_shape=grads + [jax.ShapeDtypeStruct((1, HEADS), f32)],
        in_specs=[space] * 4,
        out_specs=[far] * 3 + [space],
        scratch_shapes=[dma((3,))],
        compiler_params=pltpu.CompilerParams(vmem_limit_bytes=8 << 20),
    )(*results)
    return dq[None], dk[None], dv[None], ds[0]


def solution(mesh):
    return jax.shard_map(
        functools.partial(on_device, mesh.shape["dp"]),
        mesh=mesh,
        in_specs=(
            P("dp", "ctx", None),
            P("dp", "ctx", None),
            P("dp", "ctx", None),
            P("dp", "ctx", None),
            P("dp", "ctx"),
            P("dp", "ctx"),
            P("dp", "ctx"),
            P(),
        ),
        out_specs=(P("dp", "ctx", None), P("dp", "ctx", None), P("dp", "ctx", None), P()),
        check_vma=False,
    )
```
